32 devices in a mesh: groups: 2 (over y), region: 4 (over z), head: 4 (over x, core).
Axes of the slice: x: 2, y: 2, z: 4, core: 2. Of those that a mesh axis runs over, the one named last changes fastest.
Arguments:
- video_queries: bfloat16 [2, 4, 256, 3072], P('groups', 'region', None, 'head'), parts along dimension 0, may hold values from -6 to 6
- video_keys: bfloat16 [2, 4, 256, 3072], P('groups', 'region', None, 'head'), parts along dimension 0, may hold values from -6 to 6
- video_values: bfloat16 [2, 4, 256, 3072], P('groups', 'region', None, 'head'), parts along dimension 0, may hold values from -12 to 12
- head_window: int32 [24, 2], P('head'), may hold values from 0 to 1
- prompt_keys: bfloat16 [512, 3072], P(('groups', 'region'), 'head'), parts along dimension 0, may hold values from -10 to 10
- prompt_values: bfloat16 [512, 3072], P(('groups', 'region'), 'head'), parts along dimension 0, may hold values from -10 to 10
- text_len: int32 [2], P('groups'), parts along dimension 0, may hold values from 64 to 256
Outputs:
- attended: bfloat16 [2, 4, 256, 3072], P('groups', 'region', None, 'head'), parts along dimension 0
The draws below stay inside these ranges and needn't reach their ends.
There are 2 independent parts, one for each index of `groups`. The reference program is written for one: setup_inputs(seed, part) draws one part's arguments, and reference() takes and returns one part's arrays. A program takes and returns all parts, laid end to end along the dimension named above; an argument that names none is the same for every part. Nothing has to cross between parts.
Inputs may be any that keep to these rules, and one draw needn't show every extreme that they name: `head_window`: entry (h, 0) is head h's reach in tiles along grid rows, (h, 1) along grid columns; the window spans 2 r + 1 tiles along each. The first text_len[0] of the 256 prompt tokens are live.
All inputs are finite; a program needn't handle non-finite values.
Results may differ from the reference program's by a relative error of at most 0.0035.
Values may be sent and summed in bfloat16 or wider, within the bound.
A program may use at most 128 MiB of HBM per device.

```python
import math
import jax
import jax.numpy as jnp
from jax import lax

HEADS = 24
HEAD_DIM = 128
TEXT = 256
SLABS = 1
TILE_TOK = 256
DEV_COLS = 2
GRID_ROWS = 2
TILES = 4


def draw_entries(key):
    streams = jax.random.split(jax.random.fold_in(key, 4211), 2)
    array_shape = (SLABS, TILES, TILE_TOK, HEADS * HEAD_DIM)
    queries = 1.5 * jax.random.truncated_normal(streams[0], -4.0, 4.0, array_shape, jnp.float32)
    keys_drawn = 1.5 * jax.random.truncated_normal(streams[1], -4.0, 4.0, array_shape, jnp.float32)
    return (queries, keys_drawn)


def draw_video_queries(key, part):
    return draw_entries(key)[0].astype(jnp.bfloat16)


def draw_video_keys(key, part):
    return draw_entries(key)[1].astype(jnp.bfloat16)


def plant(values, key, low, largest):
    longest = values.shape.index(max(values.shape))
    spots = []
    for shift in (0, 1):
        where = [jax.random.randint(jax.random.fold_in(key, axis), (), 0, length) for axis, length in enumerate(values.shape)]
        where[longest] = (where[longest] + shift) % values.shape[longest]
        spots.append(tuple(where))
    return values.at[spots[0]].set(low).at[spots[1]].set(largest)


def shard_levels(stream_key, dims, shards, low, high):
    def one(dim, parts):
        heights = jax.random.uniform(jax.random.fold_in(jax.random.fold_in(stream_key, 6), dim), (parts,), jnp.float32, low / len(shards), high / len(shards))
        return jnp.repeat(jnp.exp(heights), dims[dim] // parts).reshape((-1,) + (1,) * (len(dims) - dim - 1))

    level = one(*shards[0])
    for cut in shards[1:]:
        level = level * one(*cut)
    return level


def centred(own_key, extent, width, most, pieces=(), kind=jnp.bfloat16):
    gain = shard_levels(own_key, extent, pieces, -0.22, 0.18) if pieces else 1.0
    drawn = jax.random.normal(own_key, extent, jnp.float32) * width * gain
    return jnp.minimum(jnp.maximum(drawn, -most), most).astype(kind)


def setup_inputs(seed: int = 0, part: int = 0) -> dict:
    key_of = jax.random.split(jax.random.key(seed), 8)
    part_splits = jax.random.split(jax.random.fold_in(key_of[7], part), 8)
    video_queries = draw_video_queries(jax.random.fold_in(jax.random.fold_in(key_of[7], part), 71), part)
    video_keys = draw_video_keys(jax.random.fold_in(jax.random.fold_in(key_of[7], part), 71), part)
    video_values = centred(part_splits[2], (SLABS, TILES, TILE_TOK, HEADS * HEAD_DIM), 2.0, 12.0, ((1, 4), (3, 4)))
    head_window = plant(jax.random.randint(key_of[3], (HEADS, 2), 0, 2), jax.random.fold_in(key_of[3], 1), 0, 1).astype(jnp.int32)
    prompt_keys = centred(part_splits[4], (TEXT, HEADS * HEAD_DIM), 2.0, 10.0, ((0, 4), (1, 4)))
    prompt_values = centred(part_splits[5], (TEXT, HEADS * HEAD_DIM), 2.0, 10.0, ((0, 4), (1, 4)))
    text_len = jax.random.randint(part_splits[6], (1,), TEXT // 4, TEXT + 1).astype(jnp.int32)
    return dict(video_queries=video_queries, video_keys=video_keys, video_values=video_values, head_window=head_window, prompt_keys=prompt_keys, prompt_values=prompt_values, text_len=text_len)


def reference(video_queries, video_keys, video_values, head_window, prompt_keys, prompt_values, text_len):
    score_scale = 1.0 / math.sqrt(HEAD_DIM)

    def heads_first(array_in):
        array_in = array_in.astype(jnp.float32).reshape(SLABS, GRID_ROWS, DEV_COLS, TILE_TOK, HEADS, HEAD_DIM)
        return jnp.transpose(array_in, (4, 0, 1, 2, 3, 5))

    def prompt_heads(array_in):
        return jnp.transpose(array_in.astype(jnp.float32).reshape(TEXT, HEADS, HEAD_DIM), (1, 0, 2))
    row_ids = jnp.arange(GRID_ROWS, dtype=jnp.int32)[:, None]
    col_ids = jnp.arange(DEV_COLS, dtype=jnp.int32)[None, :]
    text_live = jnp.arange(TEXT, dtype=jnp.int32) < text_len[0]

    def one_head(head_item):
        head_queries, head_keys, head_values, text_keys, text_values, head_reach = head_item
        padding = ((0, 0), (1, 1), (1, 1), (0, 0), (0, 0))
        padded_keys = jnp.pad(head_keys, padding)
        padded_values = jnp.pad(head_values, padding)
        key_list, value_list, live_list = ([], [], [])
        for row_step in (-1, 0, 1):
            for col_step in (-1, 0, 1):
                key_list.append(padded_keys[:, 1 + row_step:1 + row_step + GRID_ROWS, 1 + col_step:1 + col_step + DEV_COLS])
                value_list.append(padded_values[:, 1 + row_step:1 + row_step + GRID_ROWS, 1 + col_step:1 + col_step + DEV_COLS])
                inside = (row_ids + row_step >= 0) & (row_ids + row_step < GRID_ROWS) & (col_ids + col_step >= 0) & (col_ids + col_step < DEV_COLS)
                within = (abs(row_step) <= head_reach[0]) & (abs(col_step) <= head_reach[1])
                live_list.append(inside & within)
        near_keys = jnp.concatenate(key_list, axis=3)
        near_values = jnp.concatenate(value_list, axis=3)
        near_live = jnp.repeat(jnp.stack(live_list, axis=2), TILE_TOK, axis=2)
        near_scores = jnp.einsum('srcqd,srckd->srcqk', head_queries, near_keys) * score_scale
        near_scores = jnp.where(near_live[None, :, :, None, :], near_scores, -jnp.inf)
        text_scores = jnp.einsum('srcqd,kd->srcqk', head_queries, text_keys) * score_scale
        text_scores = jnp.where(text_live, text_scores, -jnp.inf)
        scores = jnp.concatenate([near_scores, text_scores], axis=-1)
        row_max = lax.optimization_barrier(jnp.max(scores, axis=-1, keepdims=True))
        weights = jnp.exp(scores - row_max)
        row_sum = lax.optimization_barrier(jnp.sum(weights, axis=-1, keepdims=True))
        rounded = lax.optimization_barrier(weights.astype(jnp.bfloat16)).astype(jnp.float32)
        split_at = 9 * TILE_TOK
        summed = jnp.einsum('srcqk,srckd->srcqd', rounded[..., :split_at], near_values)
        summed = summed + jnp.einsum('srcqk,kd->srcqd', rounded[..., split_at:], text_values)
        return summed / row_sum
    per_head = lax.map(one_head, (heads_first(video_queries), heads_first(video_keys), heads_first(video_values), prompt_heads(prompt_keys), prompt_heads(prompt_values), head_window))
    per_head = jnp.transpose(per_head, (1, 2, 3, 4, 0, 5)).reshape(SLABS, TILES, TILE_TOK, HEADS * HEAD_DIM)
    return per_head.astype(jnp.bfloat16)
```

```python
import functools
import math

import jax
import jax.numpy as jnp
from jax import lax
from jax.experimental import pallas as pl
from jax.experimental.pallas import tpu as pltpu
from jax.sharding import PartitionSpec as P

MESH = pl.DeviceIdType.MESH
MASKED = -1e30
VMEM_BUDGET = 24 * 2**20


def absorb(softmax_state, query_heads, block_keys, block_values, allowed):
    running_max, running_sum, weighted = softmax_state
    score_scale = 1.0 / math.sqrt(query_heads.shape[-1])
    scores = (
        jnp.einsum("sqhd,skhd->shqk", query_heads, block_keys, preferred_element_type=jnp.float32)
        * score_scale
    )
    scores = jnp.where(allowed, scores, -jnp.inf)
    new_max = jnp.maximum(running_max, jnp.max(scores, axis=-1, keepdims=True))
    weights = jnp.exp(scores - new_max)
    rescale = jnp.exp(running_max - new_max)
    running_sum = running_sum * rescale + jnp.sum(weights, axis=-1, keepdims=True)
    contribution = jnp.einsum(
        "shqk,skhd->sqhd",
        weights.astype(jnp.bfloat16),
        block_values,
        preferred_element_type=jnp.float32,
    )
    weighted = weighted * jnp.transpose(rescale, (0, 2, 1, 3)) + contribution
    return (new_max, running_sum, weighted)


def gathered(
    video_queries, video_keys, video_values, head_window, prompt_keys, prompt_values, text_len
):
    slab_count = video_queries.shape[0]
    tile_tok = video_queries.shape[2]
    features = video_queries.shape[3]
    head_count = head_window.shape[0]
    head_dim = features // head_count
    region_count = lax.axis_size("region")
    grid_cols = min(8, region_count // 2)
    position = lax.axis_index("region")
    my_row = position // grid_cols
    my_col = position % grid_cols
    reach_rows = head_window[:, 0]
    reach_cols = head_window[:, 1]
    query_heads = video_queries.reshape(slab_count, tile_tok, head_count, head_dim)
    paired = jnp.stack([video_keys, video_values])
    stat_shape = (slab_count, head_count, tile_tok, 1)
    softmax_state = (
        jnp.full(stat_shape, -1e30, jnp.float32),
        jnp.zeros(stat_shape, jnp.float32),
        jnp.zeros((slab_count, tile_tok, head_count, head_dim), jnp.float32),
    )
    shard_piece = lax.all_gather(paired, "region", axis=2, tiled=True)
    piece_count = shard_piece.shape[2]

    def one_tile(tile_slot, state_in):
        row_step = tile_slot // grid_cols - my_row
        col_step = tile_slot % grid_cols - my_col
        within = (jnp.abs(row_step) <= reach_rows) & (jnp.abs(col_step) <= reach_cols)
        tile_pair = lax.dynamic_slice_in_dim(shard_piece, tile_slot, 1, 2)
        block_keys = tile_pair[0].reshape(slab_count, tile_tok, head_count, head_dim)
        block_values = tile_pair[1].reshape(slab_count, tile_tok, head_count, head_dim)
        allowed = within.reshape(1, head_count, 1, 1)

        def take_tile(state_keep):
            return absorb(state_keep, query_heads, block_keys, block_values, allowed)

        def keep_state(state_keep):
            return state_keep

        return lax.cond(jnp.any(within), take_tile, keep_state, state_in)

    softmax_state = lax.fori_loop(0, piece_count, one_tile, softmax_state)
    live_text = text_len[0]
    prompt_piece = (
        lax.all_gather(prompt_keys, "region", axis=0, tiled=True),
        lax.all_gather(prompt_values, "region", axis=0, tiled=True),
    )
    piece_count = prompt_piece[0].shape[0]
    block_keys = prompt_piece[0].reshape(1, piece_count, head_count, head_dim)
    block_values = prompt_piece[1].reshape(1, piece_count, head_count, head_dim)
    allowed = (jnp.arange(piece_count, dtype=jnp.int32) < live_text).reshape(1, 1, 1, piece_count)
    softmax_state = absorb(softmax_state, query_heads, block_keys, block_values, allowed)
    running_max, running_sum, weighted = softmax_state
    result = weighted / jnp.transpose(running_sum, (0, 2, 1, 3))
    return result.reshape(slab_count, 1, tile_tok, features).astype(jnp.bfloat16)


def attend(queries, blocks, score_scale):
    scores = [
        lax.dot_general(
            queries, keys, (((1,), (1,)), ((), ())), preferred_element_type=jnp.float32
        )
        + bias
        for keys, _, bias in blocks
    ]
    row_max = jnp.max(functools.reduce(jnp.maximum, scores), axis=-1, keepdims=True)
    weights = [jnp.exp2((block - row_max) * (score_scale / math.log(2.0))) for block in scores]
    row_sum = jnp.sum(functools.reduce(jnp.add, weights), axis=-1, keepdims=True)
    weighted = functools.reduce(
        jnp.add,
        [
            jnp.dot(weight.astype(jnp.bfloat16), values, preferred_element_type=jnp.float32)
            for weight, (_, values, _) in zip(weights, blocks)
        ],
    )
    return (weighted * (1.0 / row_sum)).astype(jnp.bfloat16)


def exchange_kernel(
    dims,
    window_ref, text_len_ref, q_ref, k_ref, v_ref, tk_ref, tv_ref, out_ref,
    q_own, k_own, v_own, tk_own, tv_own, o_out, o_land,
    q_rest, k_rest, v_rest, tk_rest, tv_rest,
    own_send, own_recv, rest_send, rest_recv, relay_send, o_send, o_recv, local_sem,
):
    n, heads, head_dim, grid_cols = dims
    me = lax.axis_index("region")
    per_device = heads // n
    rest = heads - per_device * n
    width = per_device * head_dim
    rest_cols = pl.ds(n * width, rest * head_dim)
    half = n // 2
    score_scale = 1.0 / math.sqrt(head_dim)

    barrier = pltpu.get_barrier_semaphore()
    for step in range(1, n):
        pl.semaphore_signal(
            barrier, inc=1, device_id={"region": lax.rem(me + step, n)}, device_id_type=MESH
        )

    def columns(owner):
        return pl.ds(pl.multiple_of(owner * width, head_dim), width)

    own_pairs = ((k_ref, k_own), (q_ref, q_own), (tk_ref, tk_own), (v_ref, v_own), (tv_ref, tv_own))
    rest_pairs = ((k_ref, k_rest), (v_ref, v_rest), (tk_ref, tk_rest), (tv_ref, tv_rest))

    local = [
        pltpu.make_async_copy(src.at[:, columns(me)], dst.at[me], local_sem.at[i])
        for i, (src, dst) in enumerate(own_pairs)
    ]
    if rest:
        local += [
            pltpu.make_async_copy(src.at[:, rest_cols], dst.at[me], local_sem.at[5 + i])
            for i, (src, dst) in enumerate(rest_pairs)
        ]
        local.append(pltpu.make_async_copy(q_ref.at[:, rest_cols], q_rest, local_sem.at[9]))
    for copy in local:
        copy.start()

    def own_copy(target, source, slot, i):
        src, dst = own_pairs[i]
        return pltpu.make_async_remote_copy(
            src_ref=src.at[:, columns(target)],
            dst_ref=dst.at[source],
            send_sem=own_send.at[slot, i],
            recv_sem=own_recv.at[source, i],
            device_id={"region": target},
            device_id_type=MESH,
        )

    def rest_copy(target, source, i):
        src, dst = rest_pairs[i]
        return pltpu.make_async_remote_copy(
            src_ref=src.at[:, rest_cols],
            dst_ref=dst.at[source],
            send_sem=rest_send.at[target, i],
            recv_sem=rest_recv.at[source, i],
            device_id={"region": target},
            device_id_type=MESH,
        )

    def relay_copy(target, source, i):
        dst = rest_pairs[i][1]
        return pltpu.make_async_remote_copy(
            src_ref=dst.at[source],
            dst_ref=dst.at[source],
            send_sem=relay_send.at[source, target, i],
            recv_sem=rest_recv.at[source, i],
            device_id={"region": target},
            device_id_type=MESH,
        )

    def o_copy(target, source, slot):
        return pltpu.make_async_remote_copy(
            src_ref=o_out.at[target],
            dst_ref=o_land.at[source],
            send_sem=o_send.at[slot],
            recv_sem=o_recv.at[source],
            device_id={"region": target},
            device_id_type=MESH,
        )

    def same_half(target):
        return (me != target) & ((me < half) == (target < half))

    def relay_far(target):
        return (me < half) != (target < half)

    relays = (half - 1, half)
    order = sorted(range(1, n), key=lambda step: abs(step - half))

    pl.semaphore_wait(barrier, n - 1)
    if rest:
        for target in relays:

            @pl.when(relay_far(target))
            def _(target=target):
                for i in range(4):
                    rest_copy(target, me, i).start()

    for step in order:
        for i in range(5):
            own_copy(lax.rem(me + step, n), me, step, i).start()
    if rest:
        for target in range(n):

            @pl.when(same_half(target))
            def _(target=target):
                for i in range(4):
                    rest_copy(target, me, i).start()

        for relay in relays:
            near = range(half) if relay < half else range(half, n)
            far = range(half, n) if relay < half else range(half)

            @pl.when(me == relay)
            def _(relay=relay, near=near, far=far):
                for source in far:
                    for i in range(4):
                        rest_copy(relay, source, i).wait_recv()
                        for target in near:
                            if target != relay:
                                relay_copy(target, source, i).start()

    for copy in local:
        copy.wait()
    text_bias = jnp.where(
        lax.broadcasted_iota(jnp.int32, (1, n * tk_ref.shape[0]), 1) < text_len_ref[0], 0.0, MASKED
    )

    def tile_bias(head, tile_q, tile_k):
        rows = jnp.abs(tile_q // grid_cols - tile_k // grid_cols)
        cols = jnp.abs(tile_q % grid_cols - tile_k % grid_cols)
        within = (rows <= window_ref[head, 0]) & (cols <= window_ref[head, 1])
        return jnp.where(within, 0.0, MASKED)

    def blocks_of(keys, values, text_keys, text_values, local_head, head, tile_q):
        lanes = pl.ds(local_head * head_dim, head_dim)
        blocks = [
            (keys[t, :, lanes], values[t, :, lanes], tile_bias(head, tile_q, t)) for t in range(n)
        ]
        blocks.append(
            (
                text_keys[:, :, lanes].reshape(-1, head_dim),
                text_values[:, :, lanes].reshape(-1, head_dim),
                text_bias,
            )
        )
        return blocks

    for step in order:
        for i in range(5):
            own_copy(me, lax.rem(me + step, n), step, i).wait_recv()
    for step in order + [0]:
        tile = lax.rem(me + step, n)
        for local_head in range(per_device):
            lanes = pl.ds(local_head * head_dim, head_dim)
            result = attend(
                q_own[tile, :, lanes],
                blocks_of(
                    k_own, v_own, tk_own, tv_own, local_head, me * per_device + local_head, tile
                ),
                score_scale,
            )
            if step:
                o_out[tile, :, lanes] = result
            else:
                o_land[me, :, lanes] = result
        if step:
            o_copy(tile, me, step).start()

    if rest:
        for source in range(n):
            received = (me != source) & ((me < half) == (source < half))
            if True:

                @pl.when(received)
                def _(source=source):
                    for i in range(4):
                        rest_copy(me, source, i).wait_recv()

                @pl.when(relay_far(source) & (me != half - 1) & (me != half))
                def _(source=source):
                    for i in range(4):
                        rest_copy(me, source, i).wait_recv()

        for local_head in range(rest):
            lanes = pl.ds(local_head * head_dim, head_dim)
            out_ref[:, pl.ds(n * width + local_head * head_dim, head_dim)] = attend(
                q_rest[:, lanes],
                blocks_of(
                    k_rest, v_rest, tk_rest, tv_rest, local_head, n * per_device + local_head, me
                ),
                score_scale,
            )

    for step in order:
        o_copy(me, lax.rem(me + step, n), step).wait_recv()
    for owner in range(n):
        out_ref[:, pl.ds(owner * width, width)] = o_land[owner]

    for step in order:
        for i in range(5):
            own_copy(lax.rem(me + step, n), me, step, i).wait_send()
        o_copy(lax.rem(me + step, n), me, step).wait_send()
    if rest:
        for target in range(n):

            @pl.when(same_half(target) | (relay_far(target) & (target in relays)))
            def _(target=target):
                for i in range(4):
                    rest_copy(target, me, i).wait_send()

        for relay in relays:
            near = range(half) if relay < half else range(half, n)
            far = range(half, n) if relay < half else range(half)

            @pl.when(me == relay)
            def _(relay=relay, near=near, far=far):
                for source in far:
                    for i in range(4):
                        for target in near:
                            if target != relay:
                                relay_copy(target, source, i).wait_send()


def exchange(
    video_queries, video_keys, video_values, head_window, prompt_keys, prompt_values, text_len
):
    n = lax.axis_size("region")
    tile_tok, features = video_queries.shape[2:]
    text_tok = prompt_keys.shape[0]
    heads = head_window.shape[0]
    head_dim = features // heads
    per_device = heads // n
    width = per_device * head_dim
    rest_width = max(features - n * width, head_dim)
    grid_cols = min(8, n // 2)
    kind = video_queries.dtype
    any_spec = pl.BlockSpec(memory_space=pl.ANY)
    smem_spec = pl.BlockSpec(memory_space=pltpu.SMEM)
    tile_own = pltpu.VMEM((n, tile_tok, width), kind)
    text_own = pltpu.VMEM((n, text_tok, width), kind)
    tile_rest = pltpu.VMEM((n, tile_tok, rest_width), kind)
    text_rest = pltpu.VMEM((n, text_tok, rest_width), kind)
    dma = pltpu.SemaphoreType.DMA
    keys_total = n * (tile_tok + text_tok)
    result = pl.pallas_call(
        functools.partial(exchange_kernel, (n, heads, head_dim, grid_cols)),
        out_shape=jax.ShapeDtypeStruct((tile_tok, features), kind),
        in_specs=[smem_spec, smem_spec] + [any_spec] * 5,
        out_specs=pl.BlockSpec(memory_space=pltpu.VMEM),
        scratch_shapes=[
            tile_own, tile_own, tile_own, text_own, text_own, tile_own, tile_own,
            pltpu.VMEM((tile_tok, rest_width), kind),
            tile_rest, tile_rest, text_rest, text_rest,
            dma((n, 5)), dma((n, 5)), dma((n, 4)), dma((n, 4)), dma((n, n, 4)),
            dma((n,)), dma((n,)), dma((10,)),
        ],
        compiler_params=pltpu.CompilerParams(collective_id=0, has_side_effects=True),
        cost_estimate=pl.CostEstimate(
            flops=4 * tile_tok * features * keys_total,
            bytes_accessed=8 * tile_tok * features * n,
            transcendentals=tile_tok * heads * keys_total,
        ),
        name="exchange_attend",
    )(
        head_window,
        text_len,
        video_queries.reshape(tile_tok, features),
        video_keys.reshape(tile_tok, features),
        video_values.reshape(tile_tok, features),
        prompt_keys,
        prompt_values,
    )
    return result.reshape(video_queries.shape)


def fits(video_queries, head_window):
    n = lax.axis_size("region")
    heads = head_window.shape[0]
    slabs, tiles, tile_tok, features = video_queries.shape
    landed = 12 * n * tile_tok * features
    return (
        slabs == 1 and tiles == 1 and n % 2 == 0 and heads >= n
        and features // heads == 128 and landed < VMEM_BUDGET
    )


def shards(
    video_queries, video_keys, video_values, head_window, prompt_keys, prompt_values, text_len
):
    route = exchange if fits(video_queries, head_window) else gathered
    return route(
        video_queries, video_keys, video_values, head_window, prompt_keys, prompt_values, text_len
    )


def solution(mesh):
    in_specs = (
        P("groups", "region", None, "head"),
        P("groups", "region", None, "head"),
        P("groups", "region", None, "head"),
        P("head", None),
        P(("groups", "region"), "head"),
        P(("groups", "region"), "head"),
        P("groups"),
    )
    out_specs = P("groups", "region", None, "head")
    return jax.shard_map(shards, mesh=mesh, in_specs=in_specs, out_specs=out_specs, check_vma=False)
```

```python
import functools
import math

import jax
import jax.numpy as jnp
from jax import lax
from jax.experimental import pallas as pl
from jax.experimental.pallas import tpu as pltpu
from jax.sharding import PartitionSpec as P

MESH = pl.DeviceIdType.MESH
MASKED = -1e30
VMEM_BUDGET = 24 * 2**20


def absorb(softmax_state, query_heads, block_keys, block_values, allowed):
    running_max, running_sum, weighted = softmax_state
    score_scale = 1.0 / math.sqrt(query_heads.shape[-1])
    scores = (
        jnp.einsum("sqhd,skhd->shqk", query_heads, block_keys, preferred_element_type=jnp.float32)
        * score_scale
    )
    scores = jnp.where(allowed, scores, -jnp.inf)
    new_max = jnp.maximum(running_max, jnp.max(scores, axis=-1, keepdims=True))
    weights = jnp.exp(scores - new_max)
    rescale = jnp.exp(running_max - new_max)
    running_sum = running_sum * rescale + jnp.sum(weights, axis=-1, keepdims=True)
    contribution = jnp.einsum(
        "shqk,skhd->sqhd",
        weights.astype(jnp.bfloat16),
        block_values,
        preferred_element_type=jnp.float32,
    )
    weighted = weighted * jnp.transpose(rescale, (0, 2, 1, 3)) + contribution
    return (new_max, running_sum, weighted)


def gathered(
    video_queries, video_keys, video_values, head_window, prompt_keys, prompt_values, text_len
):
    slab_count = video_queries.shape[0]
    tile_tok = video_queries.shape[2]
    features = video_queries.shape[3]
    head_count = head_window.shape[0]
    head_dim = features // head_count
    region_count = lax.axis_size("region")
    grid_cols = min(8, region_count // 2)
    position = lax.axis_index("region")
    my_row = position // grid_cols
    my_col = position % grid_cols
    reach_rows = head_window[:, 0]
    reach_cols = head_window[:, 1]
    query_heads = video_queries.reshape(slab_count, tile_tok, head_count, head_dim)
    paired = jnp.stack([video_keys, video_values])
    stat_shape = (slab_count, head_count, tile_tok, 1)
    softmax_state = (
        jnp.full(stat_shape, -1e30, jnp.float32),
        jnp.zeros(stat_shape, jnp.float32),
        jnp.zeros((slab_count, tile_tok, head_count, head_dim), jnp.float32),
    )
    shard_piece = lax.all_gather(paired, "region", axis=2, tiled=True)
    piece_count = shard_piece.shape[2]

    def one_tile(tile_slot, state_in):
        row_step = tile_slot // grid_cols - my_row
        col_step = tile_slot % grid_cols - my_col
        within = (jnp.abs(row_step) <= reach_rows) & (jnp.abs(col_step) <= reach_cols)
        tile_pair = lax.dynamic_slice_in_dim(shard_piece, tile_slot, 1, 2)
        block_keys = tile_pair[0].reshape(slab_count, tile_tok, head_count, head_dim)
        block_values = tile_pair[1].reshape(slab_count, tile_tok, head_count, head_dim)
        allowed = within.reshape(1, head_count, 1, 1)

        def take_tile(state_keep):
            return absorb(state_keep, query_heads, block_keys, block_values, allowed)

        def keep_state(state_keep):
            return state_keep

        return lax.cond(jnp.any(within), take_tile, keep_state, state_in)

    softmax_state = lax.fori_loop(0, piece_count, one_tile, softmax_state)
    live_text = text_len[0]
    prompt_piece = (
        lax.all_gather(prompt_keys, "region", axis=0, tiled=True),
        lax.all_gather(prompt_values, "region", axis=0, tiled=True),
    )
    piece_count = prompt_piece[0].shape[0]
    block_keys = prompt_piece[0].reshape(1, piece_count, head_count, head_dim)
    block_values = prompt_piece[1].reshape(1, piece_count, head_count, head_dim)
    allowed = (jnp.arange(piece_count, dtype=jnp.int32) < live_text).reshape(1, 1, 1, piece_count)
    softmax_state = absorb(softmax_state, query_heads, block_keys, block_values, allowed)
    running_max, running_sum, weighted = softmax_state
    result = weighted / jnp.transpose(running_sum, (0, 2, 1, 3))
    return result.reshape(slab_count, 1, tile_tok, features).astype(jnp.bfloat16)


def attend(queries, blocks, score_scale):
    scores = [
        lax.dot_general(
            queries, keys, (((1,), (1,)), ((), ())), preferred_element_type=jnp.float32
        )
        + bias
        for keys, _, bias in blocks
    ]
    row_max = jnp.max(functools.reduce(jnp.maximum, scores), axis=-1, keepdims=True)
    weights = [jnp.exp2((block - row_max) * (score_scale / math.log(2.0))) for block in scores]
    row_sum = jnp.sum(functools.reduce(jnp.add, weights), axis=-1, keepdims=True)
    weighted = functools.reduce(
        jnp.add,
        [
            jnp.dot(weight.astype(jnp.bfloat16), values, preferred_element_type=jnp.float32)
            for weight, (_, values, _) in zip(weights, blocks)
        ],
    )
    return (weighted * (1.0 / row_sum)).astype(jnp.bfloat16)

def exchange_kernel(
    dims,
    window_ref, text_len_ref, q_ref, k_ref, v_ref, tk_ref, tv_ref, out_ref,
    k_own, tk_own, q_own, v_own, tv_own, o_own, o_land,
    k_ext, tk_ext, q_ext, v_ext, tv_ext, o_ext, x_land,
    own_send, own_recv, o_send, o_recv,
    ext_send, ext_recv, x_send, x_recv, local_sem,
):
    n, heads, head_dim, grid_cols = dims
    me = lax.axis_index("region")
    odd = lax.axis_index("head") % 2
    per_device = heads // n
    extra = heads - per_device * n
    width = per_device * head_dim
    half = n // 2
    side, place = me // half, me % half
    score_scale = 1.0 / math.sqrt(head_dim)
    peers = [(1 - side) * half + lax.rem(place + j, half) for j in range(half)]
    peers += [side * half + lax.rem(place + j, half) for j in range(1, half)]

    barrier = pltpu.get_barrier_semaphore()
    for peer in peers:
        pl.semaphore_signal(barrier, inc=1, device_id={"region": peer}, device_id_type=MESH)

    def extra_owner(e):
        return jnp.where(odd == 0, e, n - 1 - e)

    my_extra = jnp.where(odd == 0, me, n - 1 - me)
    inputs = (k_ref, tk_ref, q_ref, v_ref, tv_ref)
    own_bufs = (k_own, tk_own, q_own, v_own, tv_own)
    ext_bufs = (k_ext, tk_ext, q_ext, v_ext, tv_ext)
    parts = range(5)

    def own_cols(owner):
        return pl.ds(pl.multiple_of(owner * width, head_dim), width)

    def ext_cols(e):
        return pl.ds(pl.multiple_of(n * width + e * head_dim, head_dim), head_dim)

    def remote(src, dst, send_sem, recv_sem, target):
        return pltpu.make_async_remote_copy(
            src_ref=src,
            dst_ref=dst,
            send_sem=send_sem,
            recv_sem=recv_sem,
            device_id={"region": target},
            device_id_type=MESH,
        )

    def own_copy(target, source, j, i):
        return remote(
            inputs[i].at[:, own_cols(target)],
            own_bufs[i].at[source],
            own_send.at[j, i],
            own_recv.at[source, i],
            target,
        )

    def ext_copy(e, target, source, i):
        return remote(
            inputs[i].at[:, ext_cols(e)],
            ext_bufs[i].at[source],
            ext_send.at[e, i],
            ext_recv.at[source, i],
            target,
        )

    def o_copy(target, source, j):
        return remote(o_own.at[target], o_land.at[source], o_send.at[j], o_recv.at[source], target)

    def x_copy(e, target, j):
        return remote(o_ext.at[target], x_land.at[e], x_send.at[j], x_recv.at[e], target)

    local = [
        pltpu.make_async_copy(inputs[i].at[:, own_cols(me)], own_bufs[i].at[me], local_sem.at[i])
        for i in parts
    ]
    for copy in local:
        copy.start()
    local_ext = []
    if extra:
        local_ext = [
            pltpu.make_async_copy(
                inputs[i].at[:, ext_cols(lax.rem(my_extra, extra))],
                ext_bufs[i].at[me],
                local_sem.at[5 + i],
            )
            for i in parts
        ]
        for copy in local_ext:
            copy.start()

    pl.semaphore_wait(barrier, n - 1)
    for e in range(extra):

        @pl.when(me != extra_owner(e))
        def _(e=e):
            for i in parts:
                ext_copy(e, extra_owner(e), me, i).start()

    for j, peer in enumerate(peers):
        for i in parts:
            own_copy(peer, me, j, i).start()

    text_bias = jnp.where(
        lax.broadcasted_iota(jnp.int32, (1, n * tk_ref.shape[0]), 1) < text_len_ref[0], 0.0, MASKED
    )

    def tile_bias(head, tile_q, tile_k):
        rows = jnp.abs(tile_q // grid_cols - tile_k // grid_cols)
        cols = jnp.abs(tile_q % grid_cols - tile_k % grid_cols)
        within = (rows <= window_ref[0, head]) & (cols <= window_ref[1, head])
        return jnp.where(within, 0.0, MASKED)

    def tile_attend(bufs, slot, head, tile):
        keys, text_keys, queries, values, text_values = bufs
        lanes = pl.ds(slot * head_dim, head_dim)
        blocks = [(keys[t, :, lanes], values[t, :, lanes], tile_bias(head, tile, t)) for t in range(n)]
        blocks.append(
            (
                text_keys[:, :, lanes].reshape(-1, head_dim),
                text_values[:, :, lanes].reshape(-1, head_dim),
                text_bias,
            )
        )
        return attend(queries[tile, :, lanes], blocks, score_scale)

    for copy in local + local_ext:
        copy.wait()
    if extra:

        @pl.when(my_extra < extra)
        def _():
            for peer in peers:
                for i in parts:
                    ext_copy(my_extra, me, peer, i).wait_recv()
            for j, peer in enumerate(peers):
                o_ext[peer] = tile_attend(ext_bufs, 0, n * per_device + my_extra, peer)
                x_copy(my_extra, peer, j).start()
            x_land[my_extra] = tile_attend(ext_bufs, 0, n * per_device + my_extra, me)

    for peer in peers:
        for i in parts:
            own_copy(me, peer, 0, i).wait_recv()
    for j, peer in enumerate(peers):
        for slot in range(per_device):
            o_own[peer, :, pl.ds(slot * head_dim, head_dim)] = tile_attend(
                own_bufs, slot, me * per_device + slot, peer
            )
        o_copy(peer, me, j).start()
    for slot in range(per_device):
        o_land[me, :, pl.ds(slot * head_dim, head_dim)] = tile_attend(
            own_bufs, slot, me * per_device + slot, me
        )

    for e in range(extra):

        @pl.when(me != extra_owner(e))
        def _(e=e):
            x_copy(e, me, 0).wait_recv()

        out_ref[:, pl.ds(n * width + e * head_dim, head_dim)] = x_land[e]
    for peer in peers:
        o_copy(me, peer, 0).wait_recv()
    for owner in range(n):
        out_ref[:, pl.ds(owner * width, width)] = o_land[owner]

    for j, peer in enumerate(peers):
        for i in parts:
            own_copy(peer, me, j, i).wait_send()
        o_copy(peer, me, j).wait_send()
    for e in range(extra):

        @pl.when(me != extra_owner(e))
        def _(e=e):
            for i in parts:
                ext_copy(e, extra_owner(e), me, i).wait_send()

    if extra:

        @pl.when(my_extra < extra)
        def _():
            for j, peer in enumerate(peers):
                x_copy(my_extra, peer, j).wait_send()


def exchange(
    video_queries, video_keys, video_values, head_window, prompt_keys, prompt_values, text_len
):
    n = lax.axis_size("region")
    tile_tok, features = video_queries.shape[2:]
    text_tok = prompt_keys.shape[0]
    heads = head_window.shape[0]
    head_dim = features // heads
    width = heads // n * head_dim
    extra = max(heads % n, 1)
    grid_cols = min(8, n // 2)
    kind = video_queries.dtype
    any_spec = pl.BlockSpec(memory_space=pl.ANY)
    smem_spec = pl.BlockSpec(memory_space=pltpu.SMEM)
    tile_own = pltpu.VMEM((n, tile_tok, width), kind)
    text_own = pltpu.VMEM((n, text_tok, width), kind)
    tile_ext = pltpu.VMEM((n, tile_tok, head_dim), kind)
    text_ext = pltpu.VMEM((n, text_tok, head_dim), kind)
    dma = pltpu.SemaphoreType.DMA
    keys_total = n * (tile_tok + text_tok)
    result = pl.pallas_call(
        functools.partial(exchange_kernel, (n, heads, head_dim, grid_cols)),
        out_shape=jax.ShapeDtypeStruct((tile_tok, features), kind),
        in_specs=[smem_spec, smem_spec] + [any_spec] * 5,
        out_specs=pl.BlockSpec(memory_space=pltpu.VMEM),
        scratch_shapes=[
            tile_own, text_own, tile_own, tile_own, text_own, tile_own, tile_own,
            tile_ext, text_ext, tile_ext, tile_ext, text_ext, tile_ext,
            pltpu.VMEM((extra, tile_tok, head_dim), kind),
            dma((n, 5)), dma((n, 5)), dma((n,)), dma((n,)),
            dma((extra, 5)), dma((n, 5)), dma((n,)), dma((extra,)), dma((10,)),
        ],
        compiler_params=pltpu.CompilerParams(collective_id=0, has_side_effects=True),
        cost_estimate=pl.CostEstimate(
            flops=4 * tile_tok * features * keys_total,
            bytes_accessed=8 * tile_tok * features * n,
            transcendentals=tile_tok * heads * keys_total,
        ),
        name="exchange_attend",
    )(
        head_window.T,
        text_len,
        video_queries.reshape(tile_tok, features),
        video_keys.reshape(tile_tok, features),
        video_values.reshape(tile_tok, features),
        prompt_keys,
        prompt_values,
    )
    return result.reshape(video_queries.shape)


def fits(video_queries, head_window):
    n = lax.axis_size("region")
    heads = head_window.shape[0]
    slabs, tiles, tile_tok, features = video_queries.shape
    landed = 12 * n * tile_tok * features
    return (
        slabs == 1 and tiles == 1 and n % 2 == 0 and heads >= n
        and features // heads == 128 and landed < VMEM_BUDGET
    )


def shards(
    video_queries, video_keys, video_values, head_window, prompt_keys, prompt_values, text_len
):
    route = exchange if fits(video_queries, head_window) else gathered
    return route(
        video_queries, video_keys, video_values, head_window, prompt_keys, prompt_values, text_len
    )


def solution(mesh):
    in_specs = (
        P("groups", "region", None, "head"),
        P("groups", "region", None, "head"),
        P("groups", "region", None, "head"),
        P("head", None),
        P(("groups", "region"), "head"),
        P(("groups", "region"), "head"),
        P("groups"),
    )
    out_specs = P("groups", "region", None, "head")
    return jax.shard_map(shards, mesh=mesh, in_specs=in_specs, out_specs=out_specs, check_vma=False)
```

```python
import functools
import math

import jax
import jax.numpy as jnp
from jax import lax
from jax.experimental import pallas as pl
from jax.experimental.pallas import tpu as pltpu
from jax.sharding import PartitionSpec as P

MESH = pl.DeviceIdType.MESH
MASKED = -1e30
VMEM_BUDGET = 24 * 2**20


def absorb(softmax_state, query_heads, block_keys, block_values, allowed):
    running_max, running_sum, weighted = softmax_state
    score_scale = 1.0 / math.sqrt(query_heads.shape[-1])
    scores = (
        jnp.einsum("sqhd,skhd->shqk", query_heads, block_keys, preferred_element_type=jnp.float32)
        * score_scale
    )
    scores = jnp.where(allowed, scores, -jnp.inf)
    new_max = jnp.maximum(running_max, jnp.max(scores, axis=-1, keepdims=True))
    weights = jnp.exp(scores - new_max)
    rescale = jnp.exp(running_max - new_max)
    running_sum = running_sum * rescale + jnp.sum(weights, axis=-1, keepdims=True)
    contribution = jnp.einsum(
        "shqk,skhd->sqhd",
        weights.astype(jnp.bfloat16),
        block_values,
        preferred_element_type=jnp.float32,
    )
    weighted = weighted * jnp.transpose(rescale, (0, 2, 1, 3)) + contribution
    return (new_max, running_sum, weighted)


def gathered(
    video_queries, video_keys, video_values, head_window, prompt_keys, prompt_values, text_len
):
    slab_count = video_queries.shape[0]
    tile_tok = video_queries.shape[2]
    features = video_queries.shape[3]
    head_count = head_window.shape[0]
    head_dim = features // head_count
    region_count = lax.axis_size("region")
    grid_cols = min(8, region_count // 2)
    position = lax.axis_index("region")
    my_row = position // grid_cols
    my_col = position % grid_cols
    reach_rows = head_window[:, 0]
    reach_cols = head_window[:, 1]
    query_heads = video_queries.reshape(slab_count, tile_tok, head_count, head_dim)
    paired = jnp.stack([video_keys, video_values])
    stat_shape = (slab_count, head_count, tile_tok, 1)
    softmax_state = (
        jnp.full(stat_shape, -1e30, jnp.float32),
        jnp.zeros(stat_shape, jnp.float32),
        jnp.zeros((slab_count, tile_tok, head_count, head_dim), jnp.float32),
    )
    shard_piece = lax.all_gather(paired, "region", axis=2, tiled=True)
    piece_count = shard_piece.shape[2]

    def one_tile(tile_slot, state_in):
        row_step = tile_slot // grid_cols - my_row
        col_step = tile_slot % grid_cols - my_col
        within = (jnp.abs(row_step) <= reach_rows) & (jnp.abs(col_step) <= reach_cols)
        tile_pair = lax.dynamic_slice_in_dim(shard_piece, tile_slot, 1, 2)
        block_keys = tile_pair[0].reshape(slab_count, tile_tok, head_count, head_dim)
        block_values = tile_pair[1].reshape(slab_count, tile_tok, head_count, head_dim)
        allowed = within.reshape(1, head_count, 1, 1)

        def take_tile(state_keep):
            return absorb(state_keep, query_heads, block_keys, block_values, allowed)

        def keep_state(state_keep):
            return state_keep

        return lax.cond(jnp.any(within), take_tile, keep_state, state_in)

    softmax_state = lax.fori_loop(0, piece_count, one_tile, softmax_state)
    live_text = text_len[0]
    prompt_piece = (
        lax.all_gather(prompt_keys, "region", axis=0, tiled=True),
        lax.all_gather(prompt_values, "region", axis=0, tiled=True),
    )
    piece_count = prompt_piece[0].shape[0]
    block_keys = prompt_piece[0].reshape(1, piece_count, head_count, head_dim)
    block_values = prompt_piece[1].reshape(1, piece_count, head_count, head_dim)
    allowed = (jnp.arange(piece_count, dtype=jnp.int32) < live_text).reshape(1, 1, 1, piece_count)
    softmax_state = absorb(softmax_state, query_heads, block_keys, block_values, allowed)
    running_max, running_sum, weighted = softmax_state
    result = weighted / jnp.transpose(running_sum, (0, 2, 1, 3))
    return result.reshape(slab_count, 1, tile_tok, features).astype(jnp.bfloat16)


def attend(queries, blocks, score_scale):
    scores = [
        lax.dot_general(
            queries, keys, (((1,), (1,)), ((), ())), preferred_element_type=jnp.float32
        )
        + bias
        for keys, _, bias in blocks
    ]
    row_max = jnp.max(functools.reduce(jnp.maximum, scores), axis=-1, keepdims=True)
    weights = [jnp.exp2((block - row_max) * (score_scale / math.log(2.0))) for block in scores]
    row_sum = jnp.sum(functools.reduce(jnp.add, weights), axis=-1, keepdims=True)
    weighted = functools.reduce(
        jnp.add,
        [
            jnp.dot(weight.astype(jnp.bfloat16), values, preferred_element_type=jnp.float32)
            for weight, (_, values, _) in zip(weights, blocks)
        ],
    )
    return (weighted * (1.0 / row_sum)).astype(jnp.bfloat16)

def exchange_kernel(
    dims,
    window_ref, text_len_ref, q_ref, k_ref, v_ref, tk_ref, tv_ref, o_fin, x_fin,
    k_own, tk_own, v_own, tv_own, q_own, o_own, o_land,
    k_ext, tk_ext, v_ext, tv_ext, q_ext, o_ext, x_land,
    own_send, own_recv, o_send, o_recv,
    ext_send, ext_recv, x_send, x_recv, local_sem,
):
    n, heads, head_dim, grid_cols = dims
    me = lax.axis_index("region")
    odd = lax.axis_index("head") % 2
    per_device = heads // n
    extra = heads - per_device * n
    width = per_device * head_dim
    half = n // 2
    side, place = me // half, me % half
    score_scale = 1.0 / math.sqrt(head_dim)
    peers = [(1 - side) * half + lax.rem(place + j, half) for j in range(half)]
    peers += [side * half + lax.rem(place + j, half) for j in range(1, half)]

    def peer_at(j):
        across = j < half
        there = jnp.where(across, 1 - side, side)
        return there * half + lax.rem(place + jnp.where(across, j, j - half + 1), half)

    barrier = pltpu.get_barrier_semaphore()
    for peer in peers:
        pl.semaphore_signal(barrier, inc=1, device_id={"region": peer}, device_id_type=MESH)

    def extra_owner(e):
        return jnp.where(odd == 0, e, n - 1 - e)

    my_extra = jnp.where(odd == 0, me, n - 1 - me)
    inputs = (k_ref, tk_ref, v_ref, tv_ref, q_ref)
    own_bufs = (k_own, tk_own, v_own, tv_own, q_own)
    ext_bufs = (k_ext, tk_ext, v_ext, tv_ext, q_ext)
    parts, key_parts, query_part = range(5), range(4), 4

    def own_cols(owner):
        return pl.ds(pl.multiple_of(owner * width, head_dim), width)

    def ext_cols(e):
        return pl.ds(pl.multiple_of(n * width + e * head_dim, head_dim), head_dim)

    def remote(src, dst, send_sem, recv_sem, target):
        return pltpu.make_async_remote_copy(
            src_ref=src,
            dst_ref=dst,
            send_sem=send_sem,
            recv_sem=recv_sem,
            device_id={"region": target},
            device_id_type=MESH,
        )

    def own_copy(target, source, j, i):
        return remote(
            inputs[i].at[:, own_cols(target)],
            own_bufs[i].at[source],
            own_send.at[j, i],
            own_recv.at[source, i],
            target,
        )

    def ext_copy(e, target, source, i):
        return remote(
            inputs[i].at[:, ext_cols(e)],
            ext_bufs[i].at[source],
            ext_send.at[e, i],
            ext_recv.at[source, i],
            target,
        )

    def o_copy(target, source, j):
        return remote(o_own.at[target], o_land.at[source], o_send.at[j], o_recv.at[source], target)

    def x_copy(e, target, j):
        return remote(o_ext.at[target], x_land.at[e], x_send.at[j], x_recv.at[e], target)

    local = [
        pltpu.make_async_copy(inputs[i].at[:, own_cols(me)], own_bufs[i].at[me], local_sem.at[i])
        for i in parts
    ]
    for copy in local:
        copy.start()
    local_ext = []
    if extra:
        local_ext = [
            pltpu.make_async_copy(
                inputs[i].at[:, ext_cols(lax.rem(my_extra, extra))],
                ext_bufs[i].at[me],
                local_sem.at[5 + i],
            )
            for i in parts
        ]
        for copy in local_ext:
            copy.start()

    pl.semaphore_wait(barrier, n - 1)
    for j, peer in enumerate(peers):
        for i in key_parts:
            own_copy(peer, me, j, i).start()
    for j, peer in enumerate(peers):
        own_copy(peer, me, j, query_part).start()

    for pieces in (key_parts, (query_part,)):
        for e in range(extra):

            @pl.when(me != extra_owner(e))
            def _(e=e, pieces=pieces):
                for i in pieces:
                    ext_copy(e, extra_owner(e), me, i).start()


    text_bias = jnp.where(
        lax.broadcasted_iota(jnp.int32, (1, n * tk_ref.shape[0]), 1) < text_len_ref[0], 0.0, MASKED
    )

    def tile_bias(head, tile_q, tile_k):
        rows = jnp.abs(tile_q // grid_cols - tile_k // grid_cols)
        cols = jnp.abs(tile_q % grid_cols - tile_k % grid_cols)
        within = (rows <= window_ref[0, head]) & (cols <= window_ref[1, head])
        return jnp.where(within, 0.0, MASKED)

    def tile_attend(bufs, slot, head, tile):
        keys, text_keys, values, text_values, queries = bufs
        lanes = pl.ds(slot * head_dim, head_dim)
        blocks = [(keys[t, :, lanes], values[t, :, lanes], tile_bias(head, tile, t)) for t in range(n)]
        blocks.append(
            (
                text_keys[:, :, lanes].reshape(-1, head_dim),
                text_values[:, :, lanes].reshape(-1, head_dim),
                text_bias,
            )
        )
        return attend(queries[tile, :, lanes], blocks, score_scale)

    for copy in local + local_ext:
        copy.wait()
    def own_tile(out, tile):
        for slot in range(per_device):
            out[:, pl.ds(slot * head_dim, head_dim)] = tile_attend(
                own_bufs, slot, me * per_device + slot, tile
            )

    for peer in peers:
        for i in key_parts:
            own_copy(me, peer, 0, i).wait_recv()

    def own_step(j, _):
        peer = peer_at(j)

        @pl.when(j < n - 1)
        def _():
            own_copy(me, peer, 0, query_part).wait_recv()

        own_tile(o_own.at[peer], peer)

        @pl.when(j < n - 1)
        def _():
            o_copy(peer, me, j).start()

        return 0

    lax.fori_loop(0, n, own_step, 0)

    if extra:

        @pl.when(my_extra < extra)
        def _():
            head = n * per_device + my_extra
            for peer in peers:
                for i in key_parts:
                    ext_copy(my_extra, me, peer, i).wait_recv()

            def ext_step(j, _):
                peer = peer_at(j)

                @pl.when(j < n - 1)
                def _():
                    ext_copy(my_extra, me, peer, query_part).wait_recv()

                o_ext[peer] = tile_attend(ext_bufs, 0, head, peer)

                @pl.when(j < n - 1)
                def _():
                    x_copy(my_extra, peer, j).start()

                return 0

            lax.fori_loop(0, n, ext_step, 0)
            x_land[my_extra] = o_ext[me]

    for e in range(extra):

        @pl.when(me != extra_owner(e))
        def _(e=e):
            x_copy(e, me, 0).wait_recv()

        x_fin[:, pl.ds(e * head_dim, head_dim)] = x_land[e]
    for peer in peers:
        o_copy(me, peer, 0).wait_recv()
    o_land[me] = o_own[me]
    for owner in range(n):
        o_fin[:, pl.ds(owner * width, width)] = o_land[owner]

    for j, peer in enumerate(peers):
        for i in parts:
            own_copy(peer, me, j, i).wait_send()
        o_copy(peer, me, j).wait_send()
    for e in range(extra):

        @pl.when(me != extra_owner(e))
        def _(e=e):
            for i in parts:
                ext_copy(e, extra_owner(e), me, i).wait_send()

    if extra:

        @pl.when(my_extra < extra)
        def _():
            for j, peer in enumerate(peers):
                x_copy(my_extra, peer, j).wait_send()


def assemble_kernel(split, own_ref, ext_ref, out_ref):
    out_ref[:, :split] = own_ref[...]
    out_ref[:, split:] = ext_ref[:, : out_ref.shape[1] - split]


def exchange(
    video_queries, video_keys, video_values, head_window, prompt_keys, prompt_values, text_len
):
    n = lax.axis_size("region")
    tile_tok, features = video_queries.shape[2:]
    text_tok = prompt_keys.shape[0]
    heads = head_window.shape[0]
    head_dim = features // heads
    width = heads // n * head_dim
    extra = max(heads % n, 1)
    grid_cols = min(8, n // 2)
    kind = video_queries.dtype
    any_spec = pl.BlockSpec(memory_space=pl.ANY)
    smem_spec = pl.BlockSpec(memory_space=pltpu.SMEM)
    tile_own = pltpu.VMEM((n, tile_tok, width), kind)
    text_own = pltpu.VMEM((n, text_tok, width), kind)
    tile_ext = pltpu.VMEM((n, tile_tok, head_dim), kind)
    text_ext = pltpu.VMEM((n, text_tok, head_dim), kind)
    dma = pltpu.SemaphoreType.DMA
    keys_total = n * (tile_tok + text_tok)
    landed = pl.pallas_call(
        functools.partial(exchange_kernel, (n, heads, head_dim, grid_cols)),
        out_shape=(
            pltpu.VMEM((tile_tok, n * width), kind),
            pltpu.VMEM((tile_tok, extra * head_dim), kind),
        ),
        in_specs=[smem_spec, smem_spec] + [any_spec] * 5,
        out_specs=[pl.BlockSpec(memory_space=pltpu.VMEM)] * 2,
        scratch_shapes=[
            tile_own, text_own, tile_own, text_own, tile_own, tile_own, tile_own,
            tile_ext, text_ext, tile_ext, text_ext, tile_ext, tile_ext,
            pltpu.VMEM((extra, tile_tok, head_dim), kind),
            dma((n, 5)), dma((n, 5)), dma((n,)), dma((n,)),
            dma((extra, 5)), dma((n, 5)), dma((n,)), dma((extra,)), dma((10,)),
        ],
        compiler_params=pltpu.CompilerParams(collective_id=0, has_side_effects=True),
        cost_estimate=pl.CostEstimate(
            flops=4 * tile_tok * features * keys_total,
            bytes_accessed=8 * tile_tok * features * n,
            transcendentals=tile_tok * heads * keys_total,
        ),
        name="exchange_attend",
    )(
        head_window.T,
        text_len,
        video_queries.reshape(tile_tok, features),
        video_keys.reshape(tile_tok, features),
        video_values.reshape(tile_tok, features),
        prompt_keys,
        prompt_values,
    )
    result = pl.pallas_call(
        functools.partial(assemble_kernel, n * width),
        out_shape=jax.ShapeDtypeStruct((tile_tok, features), kind),
        in_specs=[pl.BlockSpec(memory_space=pltpu.VMEM)] * 2,
        out_specs=pl.BlockSpec(memory_space=pltpu.VMEM),
        name="assemble",
    )(*[pltpu.with_memory_space_constraint(piece, pltpu.VMEM) for piece in landed])
    return result.reshape(video_queries.shape)


def fits(video_queries, head_window):
    n = lax.axis_size("region")
    heads = head_window.shape[0]
    slabs, tiles, tile_tok, features = video_queries.shape
    landed = 12 * n * tile_tok * features
    return (
        slabs == 1 and tiles == 1 and n % 2 == 0 and heads >= n
        and features // heads == 128 and landed < VMEM_BUDGET
    )


def shards(
    video_queries, video_keys, video_values, head_window, prompt_keys, prompt_values, text_len
):
    route = exchange if fits(video_queries, head_window) else gathered
    return route(
        video_queries, video_keys, video_values, head_window, prompt_keys, prompt_values, text_len
    )


def solution(mesh):
    in_specs = (
        P("groups", "region", None, "head"),
        P("groups", "region", None, "head"),
        P("groups", "region", None, "head"),
        P("head", None),
        P(("groups", "region"), "head"),
        P(("groups", "region"), "head"),
        P("groups"),
    )
    out_specs = P("groups", "region", None, "head")
    return jax.shard_map(shards, mesh=mesh, in_specs=in_specs, out_specs=out_specs, check_vma=False)
```

```python
import functools
import math

import jax
import jax.numpy as jnp
from jax import lax
from jax.experimental import pallas as pl
from jax.experimental.pallas import tpu as pltpu
from jax.sharding import PartitionSpec as P

MESH = pl.DeviceIdType.MESH
MASKED = -1e30
VMEM_BUDGET = 24 * 2**20


def absorb(softmax_state, query_heads, block_keys, block_values, allowed):
    running_max, running_sum, weighted = softmax_state
    score_scale = 1.0 / math.sqrt(query_heads.shape[-1])
    scores = (
        jnp.einsum("sqhd,skhd->shqk", query_heads, block_keys, preferred_element_type=jnp.float32)
        * score_scale
    )
    scores = jnp.where(allowed, scores, -jnp.inf)
    new_max = jnp.maximum(running_max, jnp.max(scores, axis=-1, keepdims=True))
    weights = jnp.exp(scores - new_max)
    rescale = jnp.exp(running_max - new_max)
    running_sum = running_sum * rescale + jnp.sum(weights, axis=-1, keepdims=True)
    contribution = jnp.einsum(
        "shqk,skhd->sqhd",
        weights.astype(jnp.bfloat16),
        block_values,
        preferred_element_type=jnp.float32,
    )
    weighted = weighted * jnp.transpose(rescale, (0, 2, 1, 3)) + contribution
    return (new_max, running_sum, weighted)


def gathered(
    video_queries, video_keys, video_values, head_window, prompt_keys, prompt_values, text_len
):
    slab_count = video_queries.shape[0]
    tile_tok = video_queries.shape[2]
    features = video_queries.shape[3]
    head_count = head_window.shape[0]
    head_dim = features // head_count
    region_count = lax.axis_size("region")
    grid_cols = min(8, region_count // 2)
    position = lax.axis_index("region")
    my_row = position // grid_cols
    my_col = position % grid_cols
    reach_rows = head_window[:, 0]
    reach_cols = head_window[:, 1]
    query_heads = video_queries.reshape(slab_count, tile_tok, head_count, head_dim)
    paired = jnp.stack([video_keys, video_values])
    stat_shape = (slab_count, head_count, tile_tok, 1)
    softmax_state = (
        jnp.full(stat_shape, -1e30, jnp.float32),
        jnp.zeros(stat_shape, jnp.float32),
        jnp.zeros((slab_count, tile_tok, head_count, head_dim), jnp.float32),
    )
    shard_piece = lax.all_gather(paired, "region", axis=2, tiled=True)
    piece_count = shard_piece.shape[2]

    def one_tile(tile_slot, state_in):
        row_step = tile_slot // grid_cols - my_row
        col_step = tile_slot % grid_cols - my_col
        within = (jnp.abs(row_step) <= reach_rows) & (jnp.abs(col_step) <= reach_cols)
        tile_pair = lax.dynamic_slice_in_dim(shard_piece, tile_slot, 1, 2)
        block_keys = tile_pair[0].reshape(slab_count, tile_tok, head_count, head_dim)
        block_values = tile_pair[1].reshape(slab_count, tile_tok, head_count, head_dim)
        allowed = within.reshape(1, head_count, 1, 1)

        def take_tile(state_keep):
            return absorb(state_keep, query_heads, block_keys, block_values, allowed)

        def keep_state(state_keep):
            return state_keep

        return lax.cond(jnp.any(within), take_tile, keep_state, state_in)

    softmax_state = lax.fori_loop(0, piece_count, one_tile, softmax_state)
    live_text = text_len[0]
    prompt_piece = (
        lax.all_gather(prompt_keys, "region", axis=0, tiled=True),
        lax.all_gather(prompt_values, "region", axis=0, tiled=True),
    )
    piece_count = prompt_piece[0].shape[0]
    block_keys = prompt_piece[0].reshape(1, piece_count, head_count, head_dim)
    block_values = prompt_piece[1].reshape(1, piece_count, head_count, head_dim)
    allowed = (jnp.arange(piece_count, dtype=jnp.int32) < live_text).reshape(1, 1, 1, piece_count)
    softmax_state = absorb(softmax_state, query_heads, block_keys, block_values, allowed)
    running_max, running_sum, weighted = softmax_state
    result = weighted / jnp.transpose(running_sum, (0, 2, 1, 3))
    return result.reshape(slab_count, 1, tile_tok, features).astype(jnp.bfloat16)


def attend(queries, blocks, score_scale):
    scores = [
        lax.dot_general(
            queries, keys, (((1,), (1,)), ((), ())), preferred_element_type=jnp.float32
        )
        + bias
        for keys, _, bias in blocks
    ]
    row_max = jnp.max(functools.reduce(jnp.maximum, scores), axis=-1, keepdims=True)
    weights = [jnp.exp2((block - row_max) * (score_scale / math.log(2.0))) for block in scores]
    row_sum = jnp.sum(functools.reduce(jnp.add, weights), axis=-1, keepdims=True)
    weighted = functools.reduce(
        jnp.add,
        [
            jnp.dot(weight.astype(jnp.bfloat16), values, preferred_element_type=jnp.float32)
            for weight, (_, values, _) in zip(weights, blocks)
        ],
    )
    return (weighted * (1.0 / row_sum)).astype(jnp.bfloat16)

def exchange_kernel(
    dims,
    window_ref, text_len_ref, q_ref, k_ref, v_ref, tk_ref, tv_ref, o_fin, x_fin,
    k_own, tk_own, v_own, tv_own, q_own, o_own,
    k_ext, tk_ext, v_ext, tv_ext, q_ext, o_ext,
    own_send, own_recv, o_send, o_recv,
    ext_send, ext_recv, x_send, x_recv, local_sem,
):
    n, heads, head_dim, grid_cols = dims
    me = lax.axis_index("region")
    odd = lax.axis_index("head") % 2
    per_device = heads // n
    extra = heads - per_device * n
    width = per_device * head_dim
    half = n // 2
    side, place = me // half, me % half
    score_scale = 1.0 / math.sqrt(head_dim)
    peers = [(1 - side) * half + lax.rem(place + j, half) for j in range(half)]
    peers += [side * half + lax.rem(place + j, half) for j in range(1, half)]

    def peer_at(j):
        across = j < half
        there = jnp.where(across, 1 - side, side)
        return there * half + lax.rem(place + jnp.where(across, j, j - half + 1), half)

    barrier = pltpu.get_barrier_semaphore()
    for peer in peers:
        pl.semaphore_signal(barrier, inc=1, device_id={"region": peer}, device_id_type=MESH)

    def extra_owner(e):
        return jnp.where(odd == 0, e, n - 1 - e)

    my_extra = jnp.where(odd == 0, me, n - 1 - me)
    inputs = (k_ref, tk_ref, v_ref, tv_ref, q_ref)
    own_bufs = (k_own, tk_own, v_own, tv_own, q_own)
    ext_bufs = (k_ext, tk_ext, v_ext, tv_ext, q_ext)
    parts, key_parts, query_part = range(5), range(4), 4

    def own_cols(owner):
        return pl.ds(pl.multiple_of(owner * width, head_dim), width)

    def ext_cols(e):
        return pl.ds(pl.multiple_of(n * width + e * head_dim, head_dim), head_dim)

    def fin_cols(e):
        return pl.ds(pl.multiple_of(e * head_dim, head_dim), head_dim)

    def remote(src, dst, send_sem, recv_sem, target):
        return pltpu.make_async_remote_copy(
            src_ref=src,
            dst_ref=dst,
            send_sem=send_sem,
            recv_sem=recv_sem,
            device_id={"region": target},
            device_id_type=MESH,
        )

    def own_copy(target, source, j, i):
        return remote(
            inputs[i].at[:, own_cols(target)],
            own_bufs[i].at[source],
            own_send.at[j, i],
            own_recv.at[source, i],
            target,
        )

    def ext_copy(e, target, source, i):
        return remote(
            inputs[i].at[:, ext_cols(e)],
            ext_bufs[i].at[source],
            ext_send.at[e, i],
            ext_recv.at[source, i],
            target,
        )

    def o_copy(target, source, j):
        return remote(
            o_own.at[target],
            o_fin.at[:, own_cols(source)],
            o_send.at[j],
            o_recv.at[source],
            target,
        )

    def x_copy(e, target, j):
        return remote(
            o_ext.at[target], x_fin.at[:, fin_cols(e)], x_send.at[j], x_recv.at[e], target
        )

    local = [
        pltpu.make_async_copy(inputs[i].at[:, own_cols(me)], own_bufs[i].at[me], local_sem.at[i])
        for i in parts
    ]
    for copy in local:
        copy.start()
    local_ext = []
    if extra:
        local_ext = [
            pltpu.make_async_copy(
                inputs[i].at[:, ext_cols(lax.rem(my_extra, extra))],
                ext_bufs[i].at[me],
                local_sem.at[5 + i],
            )
            for i in parts
        ]
        for copy in local_ext:
            copy.start()

    pl.semaphore_wait(barrier, n - 1)
    for j, peer in enumerate(peers):
        for i in key_parts:
            own_copy(peer, me, j, i).start()
    for j, peer in enumerate(peers):
        own_copy(peer, me, j, query_part).start()

    for pieces in (key_parts, (query_part,)):
        for e in range(extra):

            @pl.when(me != extra_owner(e))
            def _(e=e, pieces=pieces):
                for i in pieces:
                    ext_copy(e, extra_owner(e), me, i).start()


    text_bias = jnp.where(
        lax.broadcasted_iota(jnp.int32, (1, n * tk_ref.shape[0]), 1) < text_len_ref[0], 0.0, MASKED
    )

    def tile_bias(head, tile_q, tile_k):
        rows = jnp.abs(tile_q // grid_cols - tile_k // grid_cols)
        cols = jnp.abs(tile_q % grid_cols - tile_k % grid_cols)
        within = (rows <= window_ref[0, head]) & (cols <= window_ref[1, head])
        return jnp.where(within, 0.0, MASKED)

    def tile_attend(bufs, slot, head, tile):
        keys, text_keys, values, text_values, queries = bufs
        lanes = pl.ds(slot * head_dim, head_dim)
        blocks = [(keys[t, :, lanes], values[t, :, lanes], tile_bias(head, tile, t)) for t in range(n)]
        blocks.append(
            (
                text_keys[:, :, lanes].reshape(-1, head_dim),
                text_values[:, :, lanes].reshape(-1, head_dim),
                text_bias,
            )
        )
        return attend(queries[tile, :, lanes], blocks, score_scale)

    for copy in local + local_ext:
        copy.wait()
    def own_tile(out, tile):
        for slot in range(per_device):
            out[:, pl.ds(slot * head_dim, head_dim)] = tile_attend(
                own_bufs, slot, me * per_device + slot, tile
            )

    for peer in peers:
        for i in key_parts:
            own_copy(me, peer, 0, i).wait_recv()

    def own_step(j, _):
        peer = peer_at(j)

        @pl.when(j < n - 1)
        def _():
            own_copy(me, peer, 0, query_part).wait_recv()

        own_tile(o_own.at[peer], peer)

        @pl.when(j < n - 1)
        def _():
            o_copy(peer, me, j).start()

        return 0

    lax.fori_loop(0, n, own_step, 0)

    if extra:

        @pl.when(my_extra < extra)
        def _():
            head = n * per_device + my_extra
            for peer in peers:
                for i in key_parts:
                    ext_copy(my_extra, me, peer, i).wait_recv()

            def ext_step(j, _):
                peer = peer_at(j)

                @pl.when(j < n - 1)
                def _():
                    ext_copy(my_extra, me, peer, query_part).wait_recv()

                o_ext[peer] = tile_attend(ext_bufs, 0, head, peer)

                @pl.when(j < n - 1)
                def _():
                    x_copy(my_extra, peer, j).start()

                return 0

            lax.fori_loop(0, n, ext_step, 0)
            x_fin[:, fin_cols(my_extra)] = o_ext[me]

    for e in range(extra):

        @pl.when(me != extra_owner(e))
        def _(e=e):
            x_copy(e, me, 0).wait_recv()

    for peer in peers:
        o_copy(me, peer, 0).wait_recv()
    o_fin[:, own_cols(me)] = o_own[me]

    for j, peer in enumerate(peers):
        for i in parts:
            own_copy(peer, me, j, i).wait_send()
        o_copy(peer, me, j).wait_send()
    for e in range(extra):

        @pl.when(me != extra_owner(e))
        def _(e=e):
            for i in parts:
                ext_copy(e, extra_owner(e), me, i).wait_send()

    if extra:

        @pl.when(my_extra < extra)
        def _():
            for j, peer in enumerate(peers):
                x_copy(my_extra, peer, j).wait_send()


def assemble_kernel(own_ref, ext_ref, out_ref, sems):
    split, features = own_ref.shape[1], out_ref.shape[1]
    copies = [pltpu.make_async_copy(own_ref, out_ref.at[:, pl.ds(0, split)], sems.at[0])]
    if features > split:
        rest = pl.ds(split, features - split)
        copies.append(pltpu.make_async_copy(ext_ref, out_ref.at[:, rest], sems.at[1]))
    for copy in copies:
        copy.start()
    for copy in copies:
        copy.wait()


def exchange(
    video_queries, video_keys, video_values, head_window, prompt_keys, prompt_values, text_len
):
    n = lax.axis_size("region")
    tile_tok, features = video_queries.shape[2:]
    text_tok = prompt_keys.shape[0]
    heads = head_window.shape[0]
    head_dim = features // heads
    width = heads // n * head_dim
    extra = max(heads % n, 1)
    grid_cols = min(8, n // 2)
    kind = video_queries.dtype
    any_spec = pl.BlockSpec(memory_space=pl.ANY)
    smem_spec = pl.BlockSpec(memory_space=pltpu.SMEM)
    tile_own = pltpu.VMEM((n, tile_tok, width), kind)
    text_own = pltpu.VMEM((n, text_tok, width), kind)
    tile_ext = pltpu.VMEM((n, tile_tok, head_dim), kind)
    text_ext = pltpu.VMEM((n, text_tok, head_dim), kind)
    dma = pltpu.SemaphoreType.DMA
    keys_total = n * (tile_tok + text_tok)
    landed = pl.pallas_call(
        functools.partial(exchange_kernel, (n, heads, head_dim, grid_cols)),
        out_shape=(
            pltpu.VMEM((tile_tok, n * width), kind),
            pltpu.VMEM((tile_tok, extra * head_dim), kind),
        ),
        in_specs=[smem_spec, smem_spec] + [any_spec] * 5,
        out_specs=[pl.BlockSpec(memory_space=pltpu.VMEM)] * 2,
        scratch_shapes=[
            tile_own, text_own, tile_own, text_own, tile_own, tile_own,
            tile_ext, text_ext, tile_ext, text_ext, tile_ext, tile_ext,
            dma((n, 5)), dma((n, 5)), dma((n,)), dma((n,)),
            dma((extra, 5)), dma((n, 5)), dma((n,)), dma((extra,)), dma((10,)),
        ],
        compiler_params=pltpu.CompilerParams(collective_id=0, has_side_effects=True),
        cost_estimate=pl.CostEstimate(
            flops=4 * tile_tok * features * keys_total,
            bytes_accessed=8 * tile_tok * features * n,
            transcendentals=tile_tok * heads * keys_total,
        ),
        name="exchange_attend",
    )(
        head_window.T,
        text_len,
        video_queries.reshape(tile_tok, features),
        video_keys.reshape(tile_tok, features),
        video_values.reshape(tile_tok, features),
        prompt_keys,
        prompt_values,
    )
    result = pl.pallas_call(
        assemble_kernel,
        out_shape=jax.ShapeDtypeStruct((tile_tok, features), kind),
        in_specs=[pl.BlockSpec(memory_space=pltpu.VMEM)] * 2,
        out_specs=any_spec,
        scratch_shapes=[dma((2,))],
        name="assemble",
    )(*[pltpu.with_memory_space_constraint(piece, pltpu.VMEM) for piece in landed])
    return result.reshape(video_queries.shape)


def fits(video_queries, head_window):
    n = lax.axis_size("region")
    heads = head_window.shape[0]
    slabs, tiles, tile_tok, features = video_queries.shape
    landed = 12 * n * tile_tok * features
    return (
        slabs == 1 and tiles == 1 and n % 2 == 0 and heads >= n
        and features // heads == 128 and landed < VMEM_BUDGET
    )


def shards(
    video_queries, video_keys, video_values, head_window, prompt_keys, prompt_values, text_len
):
    route = exchange if fits(video_queries, head_window) else gathered
    return route(
        video_queries, video_keys, video_values, head_window, prompt_keys, prompt_values, text_len
    )


def solution(mesh):
    in_specs = (
        P("groups", "region", None, "head"),
        P("groups", "region", None, "head"),
        P("groups", "region", None, "head"),
        P("head", None),
        P(("groups", "region"), "head"),
        P(("groups", "region"), "head"),
        P("groups"),
    )
    out_specs = P("groups", "region", None, "head")
    return jax.shard_map(shards, mesh=mesh, in_specs=in_specs, out_specs=out_specs, check_vma=False)
```
